128 devices in a mesh: dp: 4 (over x), expert: 32 (over z, y, core).
Axes of the slice: x: 4, y: 4, z: 4, core: 2. Of those that a mesh axis runs over, the one named last changes fastest.
Arguments:
- tokens: bfloat16 [16384, 7168], P('expert', 'dp'), may hold values from -6 to 6
- grad_out: bfloat16 [16384, 7168], P('expert', 'dp'), may hold values from -6 to 6
- route_ids: int32 [16384, 1], P('expert'), may hold values from 0 to 31; in each aligned block of 512 rows (0 to 511, 512 to 1023, ...) at most 20 rows name the same one
- gate_codes: int32 [16384, 1], P('expert'), may hold values from 1 to 255
- gate_weight: bfloat16 [32, 7168, 1024], P('expert', 'dp'), may hold values from -0.0625 to 0.0625
- up_weight: bfloat16 [32, 7168, 1024], P('expert', 'dp'), may hold values from -0.0625 to 0.0625
- down_weight: bfloat16 [32, 1024, 7168], P('expert', None, 'dp'), may hold values from -0.1875 to 0.1875
- momentum: bfloat16 [32, 1024, 7168], P('expert', None, 'dp'), may hold values from -6 to 6
Outputs:
- grad_tokens: bfloat16 [16384, 7168], P('expert', 'dp')
- new_down: bfloat16 [32, 1024, 7168], P('expert', None, 'dp')
- new_momentum: bfloat16 [32, 1024, 7168], P('expert', None, 'dp')
The draws below stay inside these ranges and needn't reach their ends.
Inputs may be any that keep to these rules, and one draw needn't show every extreme that they name: `route_ids`: each token names one expert. Among the 512 tokens of one index of the expert axis no expert is named by more than 20 tokens, a bound that some block reaches.
All inputs are finite; a program needn't handle non-finite values.
Results may differ from the reference program's by a relative error of at most 0.022.
Values may be sent and summed in bfloat16 or wider, within the bound.
A program may use at most 128 MiB of HBM per device.

```python
import math
import jax
import jax.numpy as jnp
import numpy as np
from jax import lax

D = 7168
H = 1024
TOPK = 1
TOK_DEV = 512
EXPERTS = 32
CAP = 20
TOKENS = 16384
N_DP = 4
N_EXPERT = 32


def with_ends(array, stream_key, low, top_value):
    extent = array.shape
    spot = [jax.random.randint(jax.random.fold_in(stream_key, axis), (), 0, extent[axis]) for axis in range(len(extent))]
    array = array.at[tuple(spot)].set(low)
    longest = extent.index(max(extent))
    spot[longest] = (spot[longest] + 1) % extent[longest]
    return array.at[tuple(spot)].set(top_value)


def shard_levels(own_key, shape, pieces, smallest, top_value):
    def one(axis_at, blocks):
        steps = jax.random.uniform(jax.random.fold_in(jax.random.fold_in(own_key, 6), axis_at), (blocks,), jnp.float32, smallest / len(pieces), top_value / len(pieces))
        return jnp.repeat(jnp.exp(steps), shape[axis_at] // blocks).reshape((-1,) + (1,) * (len(shape) - axis_at - 1))

    level = one(*pieces[0])
    for cut in pieces[1:]:
        level = level * one(*cut)
    return level


def deal_out(rng, own, number, rows, amount, top, limit, lean):
    order = jax.random.permutation(rng, amount)
    crowded, ordinary = load_shares(amount, rows * top, limit, lean, True), load_shares(amount, rows * top, limit, lean, False)
    places = jnp.arange(amount)

    def named(lengths, rotation):
        used = int((lengths > 0).sum())
        fixed = max(1, used // 4)
        shifted = fixed + (places - fixed + rotation * (used - fixed)) % max(1, amount - fixed)
        return jnp.zeros((amount,), jnp.int32).at[order[jnp.where(places < fixed, places, shifted)]].set(jnp.asarray(lengths, jnp.int32))

    lengths = jnp.where(number % 4 == 0, named(crowded, number // 4), named(ordinary, number - number // 4 - 1))
    mixed = jax.random.permutation(jax.random.fold_in(own, 3), amount)
    giver, taker = mixed[0:amount // 2 * 2:2], mixed[1:amount // 2 * 2:2]
    room = jnp.minimum(lengths[giver] - 1, limit - lengths[taker]) // 2
    room = jnp.where((giver == order[0]) | (taker == order[0]) | (lengths[taker] == 0), 0, jnp.maximum(room, 0))
    shifted = jax.random.randint(jax.random.fold_in(own, 4), (amount // 2,), 0, 1 << 20) % (room + 1)
    lengths = lengths.at[giver].add(-shifted).at[taker].add(shifted)
    items = jnp.searchsorted(jnp.cumsum(lengths), jnp.arange(rows * top), side="right").astype(jnp.int32)
    table = items.reshape(top, rows).T
    table = table[jax.random.permutation(jax.random.fold_in(own, 1), rows)]
    rotation = jax.random.randint(jax.random.fold_in(own, 2), (rows, 1), 0, top)
    return jnp.take_along_axis(table, (jnp.arange(top)[None, :] + rotation) % top, axis=1)


def load_shares(count, total, most, lean, full):
    weights = [(1 << 20) // math.isqrt(grade ** lean) + 1 for grade in range(1, count + 1)]
    largest = most if full else min(most, max(-(-total // count), total * weights[0] // sum(weights)))
    least = 1 if total - largest >= count - 1 else 0
    holding, spare = [largest] + [least] * (count - 1), total - largest - least * (count - 1)
    while spare > 0:
        candidates = [i for i in range(1, count) if holding[i] < largest] or [i for i in range(1, count) if holding[i] < most]
        whole, left = sum([weights[i] for i in candidates]), spare
        for i in candidates:
            extra = min(most - holding[i], max(1, left * weights[i] // whole), spare)
            holding[i] = holding[i] + extra
            spare = spare - extra
    return np.array(holding)


def bell_draw(rng, dims, spread, bound, split=(), held_as=jnp.bfloat16):
    values = jax.random.normal(rng, dims, jnp.float32) * spread
    if len(split) > 0:
        values = shard_levels(rng, dims, split, -0.22, 0.18) * values
    return jnp.clip(values, min=-bound, max=bound).astype(held_as)


def setup_inputs(seed: int = 0) -> dict:
    streams_of = jax.random.split(jax.random.key(seed), 9)
    tokens = bell_draw(streams_of[0], (TOKENS, D), 1.0, 6.0, ((0, 32), (1, 4)))
    grad_out = bell_draw(streams_of[1], (TOKENS, D), 1.0, 6.0, ((0, 32), (1, 4)))
    route_ids_keys = jax.random.split(jax.random.fold_in(streams_of[2], 1), TOKENS // TOK_DEV)
    route_ids_turns = jax.random.permutation(jax.random.fold_in(streams_of[2], 3), TOKENS // TOK_DEV)
    route_ids = jax.vmap(lambda own, number: deal_out(jax.random.fold_in(streams_of[2], 2), own, number, TOK_DEV, EXPERTS, TOPK, CAP, 2))(route_ids_keys, route_ids_turns).reshape((TOKENS, TOPK))
    gate_codes = with_ends(jax.random.randint(streams_of[3], (TOKENS, TOPK), 1, 256), jax.random.fold_in(streams_of[3], 1), 1, 255).astype(jnp.int32)
    gate_weight = bell_draw(streams_of[4], (EXPERTS, D, H), D ** -0.5, 0.0625, ((0, 32), (1, 4)))
    up_weight = bell_draw(streams_of[5], (EXPERTS, D, H), D ** -0.5, 0.0625, ((0, 32), (1, 4)))
    down_weight = bell_draw(streams_of[6], (EXPERTS, H, D), H ** -0.5, 0.1875, ((0, 32), (2, 4)))
    momentum = bell_draw(streams_of[7], (EXPERTS, H, D), 1.0, 6.0, ((0, 32), (2, 4)))
    return {"tokens": tokens, "grad_out": grad_out, "route_ids": route_ids, "gate_codes": gate_codes, "gate_weight": gate_weight, "up_weight": up_weight, "down_weight": down_weight, "momentum": momentum}


first_beta = 0.9
second_beta = 0.9
learn_rate = 0.01
decay_rate = 3.0
soft_width = 1.0

def activate(terms):
    pre_gate = terms[:, 0, :]
    pre_up = terms[:, 1, :]
    grad_hidden = terms[:, 2, :]
    sigmoid = jax.nn.sigmoid(pre_gate)
    active = pre_gate * sigmoid
    hidden = (active * pre_up).astype(jnp.bfloat16)
    d_gate = (grad_hidden * pre_up * sigmoid * (1.0 + pre_gate * (1.0 - sigmoid))).astype(jnp.bfloat16)
    d_up = (grad_hidden * active).astype(jnp.bfloat16)
    return (hidden, d_gate, d_up)

def lion_update(grad, weight_in, moment_in):
    moment = moment_in.astype(jnp.float32)
    weight = weight_in.astype(jnp.float32)
    blend = first_beta * moment + (1.0 - first_beta) * grad
    step = blend / jnp.sqrt(blend * blend + soft_width * soft_width)
    agree = jnp.maximum(step * jnp.sign(weight), 0.0)
    new_weight = (weight - learn_rate * (step + decay_rate * agree * weight)).astype(jnp.bfloat16)
    new_moment = (second_beta * moment + (1.0 - second_beta) * grad).astype(jnp.bfloat16)
    return (new_weight, new_moment)

def reference(tokens, grad_out, route_ids, gate_codes, gate_weight, up_weight, down_weight, momentum):
    slab = D // N_DP
    live = N_EXPERT * CAP
    flat_ids = route_ids.reshape(-1)
    owner = (jnp.arange(TOKENS * TOPK, dtype=jnp.int32) // TOPK).astype(jnp.int32)
    scales = gate_codes.reshape(-1).astype(jnp.float32) / 256.0

    def per_expert(total, expert):
        hits = flat_ids == expert
        order = jnp.nonzero(hits, size=live, fill_value=0)[0].astype(jnp.int32)
        valid = jnp.arange(live, dtype=jnp.int32) < jnp.sum(hits.astype(jnp.int32))
        rows = owner[order]
        x_rows = jnp.where(valid[:, None], tokens[rows].astype(jnp.float32), 0.0).astype(jnp.bfloat16)
        dy_rows = jnp.where(valid[:, None], scales[order][:, None] * grad_out[rows].astype(jnp.float32), 0.0).astype(jnp.bfloat16)
        w_gate = gate_weight[expert]
        w_up = up_weight[expert]
        w_down = down_weight[expert]
        terms = jnp.zeros((live, 3, H), jnp.float32)
        for slice_index in range(N_DP):
            start = slice_index * slab
            stop = start + slab
            gate_part = jnp.dot(x_rows[:, start:stop], w_gate[start:stop], preferred_element_type=jnp.float32)
            up_part = jnp.dot(x_rows[:, start:stop], w_up[start:stop], preferred_element_type=jnp.float32)
            back_part = jnp.dot(dy_rows[:, start:stop], w_down[:, start:stop].T, preferred_element_type=jnp.float32)
            stacked = jnp.stack([gate_part, up_part, back_part], axis=1).astype(jnp.bfloat16)
            stacked = lax.optimization_barrier(stacked)
            terms = terms + stacked.astype(jnp.float32)
        hidden, d_gate, d_up = activate(terms)
        grad_down = jnp.dot(hidden.T, dy_rows, preferred_element_type=jnp.float32)
        grad_rows = (jnp.dot(d_gate, w_gate.T, preferred_element_type=jnp.float32) + jnp.dot(d_up, w_up.T, preferred_element_type=jnp.float32)).astype(jnp.bfloat16)
        total = total.at[rows].add(jnp.where(valid[:, None], grad_rows.astype(jnp.float32), 0.0))
        new_weight, new_moment = lion_update(grad_down, w_down, momentum[expert])
        return (total, (new_weight, new_moment))
    total, outs = lax.scan(per_expert, jnp.zeros((TOKENS, D), jnp.float32), jnp.arange(N_EXPERT, dtype=jnp.int32))
    return (total.astype(jnp.bfloat16), outs[0], outs[1])
```

```python
import jax
import jax.numpy as jnp
from jax import lax
from jax.sharding import PartitionSpec as P

first_beta = 0.9
second_beta = 0.9
learn_rate = 0.01
decay_rate = 3.0
soft_width = 1.0
N_CHUNKS = 2


def activate(pre_gate, pre_up, grad_hidden):
    sigmoid = jax.nn.sigmoid(pre_gate)
    active = pre_gate * sigmoid
    hidden = (active * pre_up).astype(jnp.bfloat16)
    d_gate = (grad_hidden * pre_up * sigmoid * (1.0 + pre_gate * (1.0 - sigmoid))).astype(
        jnp.bfloat16
    )
    d_up = (grad_hidden * active).astype(jnp.bfloat16)
    return (hidden, d_gate, d_up)


def local(tokens, grad_out, route_ids, gate_codes, gate_weight, up_weight, down_weight, momentum):
    n_expert = lax.axis_size("expert")
    tok_rows, slab = tokens.shape
    top = route_ids.shape[1]
    capacity = max(2, tok_rows * top * 5 // (4 * n_expert))
    flat_ids = route_ids.reshape(-1)
    expert_iota = jnp.arange(n_expert, dtype=jnp.int32)
    onehot = (flat_ids[:, None] == expert_iota[None, :]).astype(jnp.int32)
    before = jnp.cumsum(onehot, axis=0) - onehot
    slot = jnp.sum(before * onehot, axis=1)
    target = flat_ids * capacity + slot
    slot_iota = jnp.arange(n_expert * capacity, dtype=jnp.int32)
    placed = (
        (target[None, :] == slot_iota[:, None])
        .astype(jnp.float32)
        .reshape(n_expert * capacity, tok_rows, top)
    )
    route_scale = gate_codes.astype(jnp.float32) / 256.0
    picker = jnp.sum(placed, axis=2).astype(jnp.bfloat16).reshape(n_expert, capacity, tok_rows)
    scaler = (
        jnp.sum(placed * route_scale[None, :, :], axis=2)
        .astype(jnp.bfloat16)
        .reshape(n_expert, capacity, tok_rows)
    )
    w_gate = gate_weight[0]
    w_up = up_weight[0]
    w_down = down_weight[0]
    bounds = [capacity * c // N_CHUNKS for c in range(N_CHUNKS + 1)]
    grad_down = None
    grad_tokens = None
    for c in range(N_CHUNKS):
        lo, hi = bounds[c], bounds[c + 1]
        pick_c = picker[:, lo:hi]
        scale_c = scaler[:, lo:hi]
        send_x = jnp.einsum("ecr,rd->ecd", pick_c, tokens, preferred_element_type=jnp.float32)
        send_dy = jnp.einsum("ecr,rd->ecd", scale_c, grad_out, preferred_element_type=jnp.float32)
        send = jnp.stack([send_x, send_dy], axis=1).astype(jnp.bfloat16)
        recv = lax.all_to_all(send, "expert", split_axis=0, concat_axis=0, tiled=True)
        x_rows = recv[:, 0]
        dy_rows = recv[:, 1]
        gate_part = jnp.einsum("scd,dh->sch", x_rows, w_gate, preferred_element_type=jnp.float32)
        up_part = jnp.einsum("scd,dh->sch", x_rows, w_up, preferred_element_type=jnp.float32)
        back_part = jnp.einsum("scd,hd->sch", dy_rows, w_down, preferred_element_type=jnp.float32)
        shares = lax.psum_scatter(
            jnp.stack([gate_part, up_part, back_part], axis=2).astype(jnp.bfloat16),
            "dp",
            scatter_dimension=0,
            tiled=True,
        ).astype(jnp.float32)
        hidden, d_gate, d_up = activate(shares[:, :, 0], shares[:, :, 1], shares[:, :, 2])
        gathered = lax.all_gather(
            jnp.stack([hidden, d_gate, d_up], axis=2), "dp", axis=0, tiled=True
        )
        hidden_all = gathered[:, :, 0]
        gate_all = gathered[:, :, 1]
        up_all = gathered[:, :, 2]
        part_w = jnp.einsum("sch,scd->hd", hidden_all, dy_rows, preferred_element_type=jnp.float32)
        grad_down = part_w if grad_down is None else grad_down + part_w
        rows_x = jnp.einsum(
            "sch,dh->scd", gate_all, w_gate, preferred_element_type=jnp.float32
        ) + jnp.einsum("sch,dh->scd", up_all, w_up, preferred_element_type=jnp.float32)
        back = rows_x.astype(jnp.bfloat16)
        returned = lax.all_to_all(back, "expert", split_axis=0, concat_axis=0, tiled=True)
        part_t = jnp.einsum("ecr,ecd->rd", pick_c, returned, preferred_element_type=jnp.float32)
        grad_tokens = part_t if grad_tokens is None else grad_tokens + part_t
    grad_tokens = grad_tokens.astype(jnp.bfloat16)
    moment = momentum[0].astype(jnp.float32)
    weight = w_down.astype(jnp.float32)
    blend = first_beta * moment + (1.0 - first_beta) * grad_down
    step = blend / jnp.sqrt(blend * blend + soft_width * soft_width)
    agree = jnp.maximum(step * jnp.sign(weight), 0.0)
    new_down = (weight - learn_rate * (step + decay_rate * agree * weight)).astype(jnp.bfloat16)
    new_moment = (second_beta * moment + (1.0 - second_beta) * grad_down).astype(jnp.bfloat16)
    return (grad_tokens, new_down[None], new_moment[None])


def solution(mesh):
    placed = (
        P("expert", "dp"),
        P("expert", "dp"),
        P("expert", None),
        P("expert", None),
        P("expert", "dp", None),
        P("expert", "dp", None),
        P("expert", None, "dp"),
        P("expert", None, "dp"),
    )
    return jax.shard_map(
        local,
        mesh=mesh,
        in_specs=placed,
        out_specs=(P("expert", "dp"), P("expert", None, "dp"), P("expert", None, "dp")),
        check_vma=False,
    )
```
